32 devices in a mesh: dp: 8 (over z, y), mp: 4 (over x, core).
Axes of the slice: x: 2, y: 2, z: 4, core: 2. Of those that a mesh axis runs over, the one named last changes fastest.
Arguments:
- embedded: bfloat16 [32, 64, 4096], P('dp', None, 'mp'), may hold values from -6 to 6
- targets: int32 [32, 64], P('dp'), may hold values from 0 to 65535
- labels: int32 [32], P('dp'), may hold values from 0 to 21
- counts: int32 [8], replicated, may hold values from 0 to 4, as said below
- destinations: int32 [32], P('dp'), may hold values from 0 to 15, as said below
- gain_in: float32 [4096], replicated, may hold values from 0.1 to 1.9
- w_query: bfloat16 [4096, 2048], P(None, 'mp'), may hold values from -40 to 40
- w_key: bfloat16 [4096, 1024], P(None, 'mp'), may hold values from -0.09375 to 0.09375
- w_value: bfloat16 [4096, 1024], P(None, 'mp'), may hold values from -0.09375 to 0.09375
- w_out: bfloat16 [2048, 4096], P('mp'), may hold values from -0.5 to 0.5
- gain_out: float32 [4096], replicated, may hold values from 0.1 to 1.9
- w_vocab: bfloat16 [4096, 65536], P('mp', 'dp'), may hold values from -40 to 40
- prev_probs: float32 [22], replicated, may hold values from 0.03 to 0.2
- log_weights: float32 [22], replicated, may hold values from -200 to 21000
Outputs:
- token_loss: float32 [1024], P(('dp', 'mp'))
- new_weights: float32 [22], replicated
- probs: float32 [22], replicated
The draws below stay inside these ranges and needn't reach their ends.
Inputs may be any that keep to these rules, and one draw needn't show every extreme that they name: The counts sum to 16. `destinations`: each value from 0 to 15 is held by exactly one live slot; entries of slots that are not live are meaningless.
All inputs are finite; a program needn't handle non-finite values.
Results may differ from the reference program's by a relative error of at most 0.015.
The reference program's roundings to bfloat16 on the way count: a program that leaves them out, or rounds other values in their place, can miss the bound.
Values may be sent and summed in bfloat16 or wider, within the bound.
A program may use at most 192 MiB of HBM per device.

```python
import math
import jax
import jax.numpy as jnp
from jax import lax

D = 4096
HEADS = 16
KV_HEADS = 8
HEAD_DIM = 128
VOCAB = 65536
DOMAINS = 22
SEQ_DEV = 2
SEQ_LEN = 64
SLOTS = 4
TOK_DEV = 128
N_DP = 8


def balance_plan(key):
    seeded = jax.random.fold_in(key, 91)
    key_order, key_shift, key_perm, key_fill = jax.random.split(seeded, 4)
    ordering = jax.random.permutation(key_order, N_DP)
    shifts = jax.random.randint(key_shift, (N_DP // 2,), 0, SEQ_DEV + 1)
    shifts = shifts.at[0].set(SEQ_DEV)
    paired = jnp.stack([SEQ_DEV + shifts, SEQ_DEV - shifts], axis=1).reshape(N_DP).astype(jnp.int32)
    counts = jnp.zeros((N_DP,), jnp.int32).at[ordering].set(paired)
    starts = jnp.cumsum(counts) - counts
    slot_ids = jnp.arange(N_DP * SLOTS, dtype=jnp.int32)
    device = slot_ids // SLOTS
    within = slot_ids % SLOTS
    is_live = within < counts[device]
    global_rank = jnp.minimum(starts[device] + within, N_DP * SEQ_DEV - 1)
    shuffled = jax.random.permutation(key_perm, N_DP * SEQ_DEV).astype(jnp.int32)
    filler = jax.random.randint(key_fill, (N_DP * SLOTS,), 0, N_DP * SEQ_DEV)
    destinations = jnp.where(is_live, shuffled[global_rank], filler).astype(jnp.int32)
    return (counts, destinations)


def draw_counts(key, part):
    return balance_plan(key)[0]


def draw_destinations(key, part):
    return balance_plan(key)[1]


def draw_w_query(key, part):
    key_base = jax.random.fold_in(jax.random.fold_in(key, 5), 0)
    entries = jax.random.normal(key_base, (D, HEADS * HEAD_DIM), jnp.float32) / math.sqrt(D)
    return jnp.clip(entries, -40.0, 40.0).astype(jnp.bfloat16)


def draw_w_vocab(key, part):
    key_base = jax.random.fold_in(jax.random.fold_in(key, 13), 0)
    entries = jax.random.normal(key_base, (D, VOCAB), jnp.float32) * (3.0 / math.sqrt(D))
    return jnp.clip(entries, -40.0, 40.0).astype(jnp.bfloat16)


def draw_log_weights(key, part):
    key_base = jax.random.fold_in(jax.random.fold_in(key, 17), 0)
    entries = jax.random.normal(key_base, (DOMAINS,), jnp.float32) * 20.0
    return entries


def set_ends(values, stream_key, smallest, top_value):
    longest = values.shape.index(max(values.shape))
    spots = []
    for shift in (0, 1):
        where = [jax.random.randint(jax.random.fold_in(stream_key, axis), (), 0, length) for axis, length in enumerate(values.shape)]
        where[longest] = (where[longest] + shift) % values.shape[longest]
        spots.append(tuple(where))
    return values.at[spots[0]].set(smallest).at[spots[1]].set(top_value)


def level_of(rng, shape, shards, low, top_value):
    level, own = 1.0, jax.random.fold_in(rng, 6)
    for axis_at, shards_of in shards:
        draws = jnp.exp(jax.random.uniform(jax.random.fold_in(own, axis_at), (shards_of,), jnp.float32, low / len(shards), top_value / len(shards)))
        level = level * jnp.repeat(draws, shape[axis_at] // shards_of).reshape([-1 if axis == axis_at else 1 for axis in range(len(shape))])
    return level


def gaussian(rng, dims, scale, reach, pieces=(), kind=jnp.bfloat16):
    values = scale * jax.random.normal(rng, dims, jnp.float32)
    if pieces:
        values = values * level_of(rng, dims, pieces, -0.22, 0.18)
    return jnp.clip(values, -reach, reach).astype(kind)


def setup_inputs(seed: int = 0) -> dict:
    splits = jax.random.split(jax.random.key(seed), 15)
    return {
        "embedded": gaussian(splits[0], (N_DP * SLOTS, SEQ_LEN, D), 1.0, 6.0, ((0, 8), (2, 4))),
        "targets": set_ends(jax.random.randint(splits[1], (N_DP * SLOTS, SEQ_LEN), 0, VOCAB), jax.random.fold_in(splits[1], 1), 0, VOCAB - 1).astype(jnp.int32),
        "labels": set_ends(jax.random.randint(splits[2], (N_DP * SLOTS,), 0, DOMAINS), jax.random.fold_in(splits[2], 1), 0, DOMAINS - 1).astype(jnp.int32),
        "counts": draw_counts(jax.random.fold_in(splits[14], 71), 0),
        "destinations": draw_destinations(jax.random.fold_in(splits[14], 71), 0),
        "gain_in": jnp.clip(1.0 + 0.18 * jax.random.normal(splits[5], (D,), jnp.float32), 0.1, 1.9),
        "w_query": draw_w_query(jax.random.fold_in(splits[14], 71), 0),
        "w_key": gaussian(splits[7], (D, KV_HEADS * HEAD_DIM), D ** -0.5, 0.09375, ((1, 4),)),
        "w_value": gaussian(splits[8], (D, KV_HEADS * HEAD_DIM), D ** -0.5, 0.09375, ((1, 4),)),
        "w_out": gaussian(splits[9], (HEADS * HEAD_DIM, D), (HEADS * HEAD_DIM // 16) ** -0.5, 0.5, ((0, 4),)),
        "gain_out": jnp.clip(1.0 + 0.18 * jax.random.normal(splits[10], (D,), jnp.float32), 0.1, 1.9),
        "w_vocab": draw_w_vocab(jax.random.fold_in(splits[14], 71), 0),
        "prev_probs": jnp.clip(jnp.exp(jax.random.uniform(splits[12], (DOMAINS,), jnp.float32, math.log(0.03), math.log(0.2))), 0.03, 0.2),
        "log_weights": draw_log_weights(jax.random.fold_in(splits[14], 71), 0),
    }


norm_eps = 1e-05
rope_base = 500000.0
memory_rate = 0.9
step_rate = 0.02
explore_mass = 0.005

def normalize(values, gain_vec):
    inv_rms = lax.rsqrt(lax.optimization_barrier(jnp.mean(values * values, axis=-1, keepdims=True)) + norm_eps)
    return values * inv_rms * gain_vec.astype(jnp.float32)

def rotate_halves(tensor):
    full_width = tensor.shape[-1]
    half_width = full_width // 2
    frequency = jnp.power(jnp.float32(rope_base), -jnp.arange(half_width, dtype=jnp.float32) * 2.0 / full_width)
    angles = jnp.arange(tensor.shape[1], dtype=jnp.float32)[:, None] * frequency[None, :]
    cosine = jnp.cos(angles)[None, :, None, :]
    sine_part = jnp.sin(angles)[None, :, None, :]
    first_half = tensor[..., :half_width]
    second = tensor[..., half_width:]
    return jnp.concatenate([first_half * cosine - second * sine_part, second * cosine + first_half * sine_part], axis=-1)

def reference(embedded, targets, labels, counts, destinations, gain_in, w_query, w_key, w_value, w_out, gain_out, w_vocab, prev_probs, log_weights):
    slot_ids = jnp.arange(N_DP * SLOTS, dtype=jnp.int32)
    is_live = slot_ids % SLOTS < counts[slot_ids // SLOTS]
    outputs = jnp.arange(N_DP * SEQ_DEV, dtype=jnp.int32)
    chosen = is_live[None, :] & (destinations[None, :] == outputs[:, None])
    source = lax.optimization_barrier(jnp.sum(jnp.where(chosen, slot_ids[None, :], 0), axis=1)).astype(jnp.int32)
    sequence_rows = embedded[source]
    seq_targets = targets[source]
    seq_labels = labels[source]
    groups = N_DP * SEQ_DEV
    tokens = groups * SEQ_LEN
    flat_rows = sequence_rows.reshape(tokens, D).astype(jnp.float32)
    normed = normalize(flat_rows, gain_in).astype(jnp.bfloat16)
    query_heads = jnp.dot(normed, w_query, preferred_element_type=jnp.float32).reshape(groups, SEQ_LEN, HEADS, HEAD_DIM)
    key_heads = jnp.dot(normed, w_key, preferred_element_type=jnp.float32).reshape(groups, SEQ_LEN, KV_HEADS, HEAD_DIM)
    value_heads = jnp.dot(normed, w_value, preferred_element_type=jnp.float32).astype(jnp.bfloat16).reshape(groups, SEQ_LEN, KV_HEADS, HEAD_DIM)
    query_heads = rotate_halves(query_heads).astype(jnp.bfloat16)
    key_heads = rotate_halves(key_heads).astype(jnp.bfloat16)
    group_size = HEADS // KV_HEADS
    key_heads = jnp.repeat(key_heads, group_size, axis=2)
    value_heads = jnp.repeat(value_heads, group_size, axis=2)
    scores = jnp.einsum('sqhe,skhe->shqk', query_heads.astype(jnp.float32), key_heads.astype(jnp.float32)) * HEAD_DIM ** (-0.5)
    causal = jnp.arange(SEQ_LEN)[:, None] >= jnp.arange(SEQ_LEN)[None, :]
    scores = jnp.where(causal[None, None], scores, -jnp.inf)
    weights = jax.nn.softmax(scores, axis=-1).astype(jnp.bfloat16)
    mixed_heads = jnp.einsum('shqk,skhe->sqhe', weights.astype(jnp.float32), value_heads.astype(jnp.float32))
    mixed_heads = mixed_heads.astype(jnp.bfloat16).reshape(tokens, HEADS * HEAD_DIM)
    update = jnp.dot(mixed_heads, w_out, preferred_element_type=jnp.float32)
    hidden = flat_rows + update
    final_rows = normalize(hidden, gain_out).astype(jnp.bfloat16)
    token_targets = seq_targets.reshape(tokens)
    block_size = TOK_DEV
    block_count = tokens // block_size

    def block_loss(inputs):
        row_block, goal_ids = inputs
        logits = jnp.dot(row_block, w_vocab, preferred_element_type=jnp.float32)
        row_top = lax.optimization_barrier(jnp.max(logits, axis=1))
        spread = lax.optimization_barrier(jnp.sum(jnp.exp(logits - row_top[:, None]), axis=1))
        picked = jnp.take_along_axis(logits, goal_ids[:, None].astype(jnp.int32), axis=1)[:, 0]
        return row_top + jnp.log(spread) - picked
    losses = lax.map(block_loss, (final_rows.reshape(block_count, block_size, D), token_targets.reshape(block_count, block_size)))
    losses = losses.reshape(tokens)
    token_labels = jnp.repeat(seq_labels, SEQ_LEN)
    member = (token_labels[:, None] == jnp.arange(DOMAINS, dtype=jnp.int32)[None, :]).astype(jnp.float32)
    loss_sums = lax.optimization_barrier(jnp.sum(member * losses[:, None], axis=0))
    token_tally = lax.optimization_barrier(jnp.sum(member, axis=0))
    reward = loss_sums / jnp.maximum(token_tally, 1.0) / prev_probs
    new_weights = memory_rate * log_weights + (1.0 - memory_rate) * reward
    probs = (1.0 - DOMAINS * explore_mass) * jax.nn.softmax(step_rate * new_weights) + explore_mass
    return (losses, new_weights, probs)
```

```python
import jax
import jax.numpy as jnp
from jax import lax
from jax.sharding import PartitionSpec as P

HEAD_DIM = 128
DOMAINS = 22
CHUNKS = 4

norm_eps = 1e-05
rope_base = 500000.0
memory_rate = 0.9
step_rate = 0.02
explore_mass = 0.005


def rotate_halves(tensor):
    full_width = tensor.shape[-1]
    half_width = full_width // 2
    frequency = jnp.power(
        jnp.float32(rope_base), -jnp.arange(half_width, dtype=jnp.float32) * 2.0 / full_width
    )
    angles = jnp.arange(tensor.shape[1], dtype=jnp.float32)[:, None] * frequency[None, :]
    cosine = jnp.cos(angles)[None, :, None, :]
    sine_part = jnp.sin(angles)[None, :, None, :]
    first_half = tensor[..., :half_width]
    second = tensor[..., half_width:]
    return jnp.concatenate(
        [first_half * cosine - second * sine_part, second * cosine + first_half * sine_part],
        axis=-1,
    )


def attend(full_rows, gain_in, w_query, w_key, w_value, seqs, seq_len):
    values = full_rows.astype(jnp.float32)
    inv_rms = lax.rsqrt(jnp.mean(values * values, axis=-1, keepdims=True) + norm_eps)
    normed = (values * inv_rms * gain_in).astype(jnp.bfloat16)
    local_heads = w_query.shape[1] // HEAD_DIM
    local_groups = w_key.shape[1] // HEAD_DIM
    group_size = local_heads // local_groups
    query = jnp.dot(normed, w_query, preferred_element_type=jnp.float32)
    key = jnp.dot(normed, w_key, preferred_element_type=jnp.float32)
    value = jnp.dot(normed, w_value, preferred_element_type=jnp.float32).astype(jnp.bfloat16)
    query = rotate_halves(query.reshape(seqs, seq_len, local_heads, HEAD_DIM))
    key = rotate_halves(key.reshape(seqs, seq_len, local_groups, HEAD_DIM))
    query = query.astype(jnp.bfloat16).reshape(seqs, seq_len, local_groups, group_size, HEAD_DIM)
    key = key.astype(jnp.bfloat16)
    value = value.reshape(seqs, seq_len, local_groups, HEAD_DIM)
    scores = jnp.einsum(
        "sqgre,skge->sgrqk", query, key, preferred_element_type=jnp.float32
    ) * HEAD_DIM ** (-0.5)
    causal = jnp.arange(seq_len)[:, None] >= jnp.arange(seq_len)[None, :]
    scores = jnp.where(causal, scores, -jnp.inf)
    weights = jax.nn.softmax(scores, axis=-1).astype(jnp.bfloat16)
    mixed = jnp.einsum("sgrqk,skge->sqgre", weights, value, preferred_element_type=jnp.float32)
    return mixed.astype(jnp.bfloat16).reshape(seqs * seq_len, local_heads * HEAD_DIM)


def local(
    embedded,
    targets,
    labels,
    counts,
    destinations,
    gain_in,
    w_query,
    w_key,
    w_value,
    w_out,
    gain_out,
    w_vocab,
    prev_probs,
    log_weights,
):
    dp = lax.axis_size("dp")
    mp = lax.axis_size("mp")
    data_index = lax.axis_index("dp")
    model_index = lax.axis_index("mp")
    chip = model_index // 2
    core = model_index % 2
    slots, seq_len, width = embedded.shape
    sequences = dp * slots // 2
    tokens = sequences * seq_len
    sibling = [(i, i ^ 1) for i in range(mp)]
    vocab_local = w_vocab.shape[1]
    columns = vocab_local // 2

    own_columns = lax.dynamic_slice_in_dim(w_vocab, core * columns, columns, 1)
    given_columns = lax.dynamic_slice_in_dim(w_vocab, (1 - core) * columns, columns, 1)
    taken_columns = lax.ppermute(given_columns, "mp", sibling)

    packed = jnp.concatenate([targets, labels[:, None], destinations[:, None]], axis=1)
    packed_all = lax.all_gather(packed, "dp", axis=0, tiled=True)
    slot_ids = jnp.arange(dp * slots, dtype=jnp.int32)
    is_live = slot_ids % slots < counts[slot_ids // slots]
    wanted = jnp.arange(sequences, dtype=jnp.int32)
    chosen = (packed_all[:, seq_len + 1][None, :] == wanted[:, None]) & is_live[None, :]
    source = jnp.sum(jnp.where(chosen, slot_ids[None, :], 0), axis=1).astype(jnp.int32)
    picked_ints = jnp.sum(jnp.where(chosen[:, :, None], packed_all[None], 0), axis=1)
    seq_targets = picked_ints[:, :seq_len]
    seq_labels = picked_ints[:, seq_len]

    flat = embedded.reshape(slots * seq_len, width)
    full_rows = lax.all_gather(flat, "mp", axis=1, tiled=True)
    mixed = attend(full_rows, gain_in, w_query, w_key, w_value, slots, seq_len)
    partial = jnp.dot(mixed, w_out, preferred_element_type=jnp.float32).astype(jnp.bfloat16)
    update = lax.psum_scatter(partial, "mp", scatter_dimension=1, tiled=True)
    hidden = flat.astype(jnp.float32) + update.astype(jnp.float32)
    squares = lax.psum(jnp.sum(hidden * hidden, axis=-1, keepdims=True), "mp") / (width * mp)
    gain_part = lax.dynamic_slice_in_dim(gain_out, model_index * width, width, 0)
    final = (hidden * lax.rsqrt(squares + norm_eps) * gain_part).astype(jnp.bfloat16)
    everyone = lax.all_gather(final.reshape(slots, seq_len, width), "dp", axis=0, tiled=True)

    chips = mp // 2
    seq_part = sequences // chips
    order = jnp.roll(source, -chip * seq_part)
    rows = jnp.concatenate(
        [lax.dynamic_index_in_dim(everyone, order[i], 0, keepdims=True) for i in range(sequences)]
    ).reshape(tokens, width)
    their_rows = lax.ppermute(rows, "mp", sibling)
    part = tokens // chips
    goals = jnp.roll(seq_targets, -chip * seq_part, axis=0)[:seq_part].reshape(part)
    goals = goals - (data_index * vocab_local + core * columns)

    def product(lhs, other, start, size):
        return jnp.dot(
            lhs, own_columns[:, start : start + size], preferred_element_type=jnp.float32
        ) + jnp.dot(
            other, taken_columns[:, start : start + size], preferred_element_type=jnp.float32
        )

    size = columns // CHUNKS
    arrived = []
    for i in range(CHUNKS):
        hops = []
        for hop in range(1, chips):
            there = slice(hop * part, (hop + 1) * part)
            outgoing = product(rows[there], their_rows[there], i * size, size)
            across = [(j, (j + 2 * hop) % mp) for j in range(mp)]
            hops.append(lax.ppermute(outgoing.astype(jnp.bfloat16), "mp", across))
        arrived.append(hops)
    tops, spreads, picks = [], [], []
    for i in range(CHUNKS):
        logits = product(rows[:part], their_rows[:part], i * size, size)
        for piece in arrived[i]:
            logits = logits + piece.astype(jnp.float32)
        top = jnp.max(logits, axis=1)
        tops.append(top)
        spreads.append(jnp.sum(jnp.exp(logits - top[:, None]), axis=1))
        ids = i * size + jnp.arange(size, dtype=jnp.int32)
        picks.append(jnp.sum(jnp.where(ids[None, :] == goals[:, None], logits, 0.0), axis=1))
    stats = jnp.stack(tops + spreads + picks)
    stats_all = lax.all_gather(stats, ("dp", "mp"), axis=0, tiled=False)
    stats_all = stats_all.reshape(dp, chips, 2, 3, CHUNKS, part)
    top_all = jnp.max(stats_all[:, :, :, 0], axis=(0, 2, 3))
    scale = jnp.exp(stats_all[:, :, :, 0] - top_all[None, :, None, None])
    spread_all = jnp.sum(stats_all[:, :, :, 1] * scale, axis=(0, 2, 3))
    picked_all = jnp.sum(stats_all[:, :, :, 2], axis=(0, 2, 3))
    losses = (top_all + jnp.log(spread_all) - picked_all).reshape(tokens)

    block = tokens // (dp * mp)
    own_loss = lax.dynamic_slice_in_dim(
        losses, (data_index * mp + model_index) * block, block, 0
    )
    domains = jnp.arange(DOMAINS, dtype=jnp.int32)
    member = (seq_labels[:, None] == domains[None, :]).astype(jnp.float32)
    per_sequence = jnp.sum(losses.reshape(sequences, seq_len), axis=1)
    loss_sums = jnp.sum(member * per_sequence[:, None], axis=0)
    token_tally = jnp.sum(member, axis=0) * seq_len
    reward = loss_sums / jnp.maximum(token_tally, 1.0) / prev_probs
    new_weights = memory_rate * log_weights + (1.0 - memory_rate) * reward
    probs = (1.0 - DOMAINS * explore_mass) * jax.nn.softmax(step_rate * new_weights) + explore_mass
    return (own_loss, new_weights, probs)


def solution(mesh):
    placed = (
        P("dp", None, "mp"),
        P("dp", None),
        P("dp"),
        P(),
        P("dp"),
        P(),
        P(None, "mp"),
        P(None, "mp"),
        P(None, "mp"),
        P("mp", None),
        P(),
        P("mp", "dp"),
        P(),
        P(),
    )
    return jax.shard_map(
        local, mesh=mesh, in_specs=placed, out_specs=(P(("dp", "mp")), P(), P()), check_vma=False
    )
```

```python
import functools

import jax
import jax.numpy as jnp
from jax import lax
from jax.experimental import pallas as pl
from jax.experimental.pallas import tpu as pltpu
from jax.sharding import PartitionSpec as P

HEAD_DIM = 128
DOMAINS = 22
PIECES = 4
MESH = pl.DeviceIdType.MESH
VMEM = pl.BlockSpec(memory_space=pltpu.VMEM)

norm_eps = 1e-05
rope_base = 500000.0
memory_rate = 0.9
step_rate = 0.02
explore_mass = 0.005


def rotate_halves(tensor):
    full_width = tensor.shape[-1]
    half_width = full_width // 2
    frequency = jnp.power(
        jnp.float32(rope_base), -jnp.arange(half_width, dtype=jnp.float32) * 2.0 / full_width
    )
    angles = jnp.arange(tensor.shape[1], dtype=jnp.float32)[:, None] * frequency[None, :]
    cosine = jnp.cos(angles)[None, :, None, :]
    sine_part = jnp.sin(angles)[None, :, None, :]
    first_half = tensor[..., :half_width]
    second = tensor[..., half_width:]
    return jnp.concatenate(
        [first_half * cosine - second * sine_part, second * cosine + first_half * sine_part],
        axis=-1,
    )


def attend(full_rows, gain_in, w_query, w_key, w_value, seqs, seq_len):
    values = full_rows.astype(jnp.float32)
    inv_rms = lax.rsqrt(jnp.mean(values * values, axis=-1, keepdims=True) + norm_eps)
    normed = (values * inv_rms * gain_in).astype(jnp.bfloat16)
    local_heads = w_query.shape[1] // HEAD_DIM
    local_groups = w_key.shape[1] // HEAD_DIM
    group_size = local_heads // local_groups
    query = jnp.dot(normed, w_query, preferred_element_type=jnp.float32)
    key = jnp.dot(normed, w_key, preferred_element_type=jnp.float32)
    value = jnp.dot(normed, w_value, preferred_element_type=jnp.float32).astype(jnp.bfloat16)
    query = rotate_halves(query.reshape(seqs, seq_len, local_heads, HEAD_DIM))
    key = rotate_halves(key.reshape(seqs, seq_len, local_groups, HEAD_DIM))
    query = query.astype(jnp.bfloat16).reshape(seqs, seq_len, local_groups, group_size, HEAD_DIM)
    key = key.astype(jnp.bfloat16)
    value = value.reshape(seqs, seq_len, local_groups, HEAD_DIM)
    scores = jnp.einsum(
        "sqgre,skge->sgrqk", query, key, preferred_element_type=jnp.float32
    ) * HEAD_DIM ** (-0.5)
    causal = jnp.arange(seq_len)[:, None] >= jnp.arange(seq_len)[None, :]
    scores = jnp.where(causal, scores, -jnp.inf)
    weights = jax.nn.softmax(scores, axis=-1).astype(jnp.bfloat16)
    mixed = jnp.einsum("sgrqk,skge->sqgre", weights, value, preferred_element_type=jnp.float32)
    return mixed.astype(jnp.bfloat16).reshape(seqs * seq_len, local_heads * HEAD_DIM)


def remote(src, dst, send_sem, recv_sem, device):
    return pltpu.make_async_remote_copy(
        src_ref=src,
        dst_ref=dst,
        send_sem=send_sem,
        recv_sem=recv_sem,
        device_id=device,
        device_id_type=MESH,
    )


def greet(peers):
    barrier = pltpu.get_barrier_semaphore()
    for peer in peers:
        pl.semaphore_signal(barrier, inc=1, device_id=peer, device_id_type=MESH)
    pl.semaphore_wait(barrier, len(peers))


def features_kernel(
    dp, mp, x_ref, ints_ref, full_ref, all_ints_ref,
    across_send, across_recv, side_send, side_recv, int_send, int_recv, local_sem,
):
    d, m = lax.axis_index("dp"), lax.axis_index("mp")
    chips = mp // 2
    chip, core = m // 2, m % 2
    sibling = (d, chip * 2 + (1 - core))
    rows, width = x_ref.shape
    size = rows // PIECES
    far = [(d, lax.rem(chip + hop, chips) * 2 + core) for hop in range(1, chips)]
    around = [(lax.rem(d + k, dp), m) for k in range(1, dp)]
    greet([sibling] + far + around)

    def place(block, piece):
        start = pl.multiple_of(block * width, width)
        return full_ref.at[pl.ds(piece * size, size), pl.ds(start, width)]

    waits = []
    for piece in range(PIECES):
        for hop in range(1, chips):
            copy = remote(
                x_ref.at[pl.ds(piece * size, size)], place(m, piece),
                across_send.at[hop - 1, piece], across_recv.at[hop - 1, piece], far[hop - 1],
            )
            copy.start()
            waits.append(copy)
    sides = []
    for piece in range(PIECES):
        copy = remote(
            x_ref.at[pl.ds(piece * size, size)], place(m, piece),
            side_send.at[0, piece], side_recv.at[0, piece], sibling,
        )
        copy.start()
        sides.append(copy)
    ints = []
    for k in range(1, dp):
        copy = remote(
            ints_ref, all_ints_ref.at[d], int_send.at[k - 1], int_recv.at[k - 1], around[k - 1]
        )
        copy.start()
        ints.append(copy)
    locals_ = [
        pltpu.make_async_copy(ints_ref, all_ints_ref.at[d], local_sem.at[0]),
        pltpu.make_async_copy(
            x_ref, full_ref.at[:, pl.ds(pl.multiple_of(m * width, width), width)], local_sem.at[1]
        ),
    ]
    for copy in locals_:
        copy.start()
    at = 0
    for piece in range(PIECES):
        for hop in range(1, chips):
            waits[at].wait_recv()
            at += 1
            origin = lax.rem(chip + chips - hop, chips) * 2 + core
            copy = remote(
                place(origin, piece), place(origin, piece),
                side_send.at[hop, piece], side_recv.at[hop, piece], sibling,
            )
            copy.start()
            sides.append(copy)
    for copy in waits:
        copy.wait_send()
    for copy in sides + ints + locals_:
        copy.wait()


def gather_features(flat, ints, dp, mp):
    rows, width = flat.shape
    chips = mp // 2
    dma = pltpu.SemaphoreType.DMA
    return pl.pallas_call(
        functools.partial(features_kernel, dp, mp),
        out_shape=(
            jax.ShapeDtypeStruct((rows, width * mp), flat.dtype),
            jax.ShapeDtypeStruct((dp,) + ints.shape, ints.dtype),
        ),
        in_specs=[VMEM] * 2,
        out_specs=(VMEM, VMEM),
        scratch_shapes=[
            dma((chips - 1, PIECES)), dma((chips - 1, PIECES)),
            dma((chips, PIECES)), dma((chips, PIECES)),
            dma((dp - 1,)), dma((dp - 1,)), dma((2,)),
        ],
        compiler_params=pltpu.CompilerParams(collective_id=0, has_side_effects=True),
        name="features",
    )(flat, ints)


def output_kernel(
    mp, mixed_ref, w_ref, own_ref, gain_ref, final_ref,
    side_out, side_in, far_out, far_in, kept, total, square_out, square_in,
    side_send, side_recv, far_send, far_recv, square_send, square_recv,
):
    d, m = lax.axis_index("dp"), lax.axis_index("mp")
    chips = mp // 2
    chip, core = m // 2, m % 2
    sibling = (d, chip * 2 + (1 - core))
    rows, width = own_ref.shape
    size = rows // PIECES
    peers = [(d, lax.rem(m + k, mp)) for k in range(1, mp)]
    greet(peers)
    hops = list(range(1, chips)) + [0]
    target = [lax.rem(chip + hop, chips) for hop in range(chips)]

    def product(block):
        start = pl.multiple_of(block * width, width)
        return jnp.dot(
            mixed_ref[...], w_ref[:, pl.ds(start, width)], preferred_element_type=jnp.float32
        )

    def cut(piece):
        return pl.ds(piece * size, size)

    sides = {}
    for hop in hops:
        side_out[hop] = product(target[hop] * 2 + (1 - core)).astype(jnp.bfloat16)
        for piece in range(PIECES):
            sides[hop, piece] = remote(
                side_out.at[hop, cut(piece)], side_in.at[hop, cut(piece)],
                side_send.at[hop, piece], side_recv.at[hop, piece], sibling,
            )
            sides[hop, piece].start()
    for hop in hops:
        kept[hop] = product(target[hop] * 2 + core)
    fars = {}
    for piece in range(PIECES):
        for hop in range(1, chips):
            sides[hop, piece].wait_recv()
            far_out[hop - 1, cut(piece)] = (
                kept[hop, cut(piece)] + side_in[hop, cut(piece)].astype(jnp.float32)
            ).astype(jnp.bfloat16)
            fars[hop, piece] = remote(
                far_out.at[hop - 1, cut(piece)], far_in.at[hop - 1, cut(piece)],
                far_send.at[hop - 1, piece], far_recv.at[hop - 1, piece],
                (d, target[hop] * 2 + core),
            )
            fars[hop, piece].start()
    for piece in range(PIECES):
        sides[0, piece].wait_recv()
        value = kept[0, cut(piece)] + side_in[0, cut(piece)].astype(jnp.float32)
        for hop in range(1, chips):
            fars[hop, piece].wait_recv()
            value = value + far_in[hop - 1, cut(piece)].astype(jnp.float32)
        total[cut(piece)] = value + own_ref[cut(piece)].astype(jnp.float32)
    hidden = total[...]
    squares = jnp.sum(hidden * hidden, axis=1, keepdims=True)
    square_out[...] = jnp.transpose(jnp.broadcast_to(squares, (rows, 128)))[:8]
    swaps = []
    for k in range(1, mp):
        copy = remote(
            square_out, square_in.at[k - 1],
            square_send.at[k - 1], square_recv.at[k - 1], peers[k - 1],
        )
        copy.start()
        swaps.append(copy)
    for copy in swaps:
        copy.wait()
    summed = square_out[...]
    for k in range(mp - 1):
        summed = summed + square_in[k]
    inverse = lax.rsqrt(summed / (width * mp) + norm_eps)
    inverse = jnp.transpose(jnp.concatenate([inverse] * 16, axis=0))[:, :1]
    final_ref[...] = (total[...] * inverse * gain_ref[...]).astype(final_ref.dtype)
    for copy in list(sides.values()) + list(fars.values()):
        copy.wait_send()


def project_output(mixed, w_out, own, gain_part, mp):
    rows, width = own.shape
    chips = mp // 2
    dma = pltpu.SemaphoreType.DMA
    half = jnp.bfloat16
    return pl.pallas_call(
        functools.partial(output_kernel, mp),
        out_shape=jax.ShapeDtypeStruct(own.shape, half),
        in_specs=[VMEM] * 4,
        out_specs=VMEM,
        scratch_shapes=[
            pltpu.VMEM((chips, rows, width), half),
            pltpu.VMEM((chips, rows, width), half),
            pltpu.VMEM((chips - 1, rows, width), half),
            pltpu.VMEM((chips - 1, rows, width), half),
            pltpu.VMEM((chips, rows, width), jnp.float32),
            pltpu.VMEM((rows, width), jnp.float32),
            pltpu.VMEM((8, rows), jnp.float32),
            pltpu.VMEM((mp - 1, 8, rows), jnp.float32),
            dma((chips, PIECES)), dma((chips, PIECES)),
            dma((chips - 1, PIECES)), dma((chips - 1, PIECES)),
            dma((mp - 1,)), dma((mp - 1,)),
        ],
        compiler_params=pltpu.CompilerParams(collective_id=1, has_side_effects=True),
        name="output",
    )(mixed, w_out, own, gain_part)


def stats_kernel(dp, mp, x_ref, all_ref, dp_send, dp_recv, mp_send, mp_recv, local_sem):
    d, m = lax.axis_index("dp"), lax.axis_index("mp")
    around = [(lax.rem(d + k, dp), m) for k in range(1, dp)]
    beside = [(d, lax.rem(m + k, mp)) for k in range(1, mp)]
    greet(around + beside)
    first = []
    for k in range(1, dp):
        copy = remote(
            x_ref, all_ref.at[m, d], dp_send.at[k - 1], dp_recv.at[k - 1], around[k - 1]
        )
        copy.start()
        first.append(copy)
    here = pltpu.make_async_copy(x_ref, all_ref.at[m, d], local_sem)
    here.start()
    here.wait()
    for copy in first:
        copy.wait()
    second = []
    for k in range(1, mp):
        copy = remote(
            all_ref.at[m], all_ref.at[m], mp_send.at[k - 1], mp_recv.at[k - 1], beside[k - 1]
        )
        copy.start()
        second.append(copy)
    for copy in second:
        copy.wait()


def gather_stats(stats, dp, mp):
    dma = pltpu.SemaphoreType.DMA
    return pl.pallas_call(
        functools.partial(stats_kernel, dp, mp),
        out_shape=jax.ShapeDtypeStruct((mp, dp) + stats.shape, stats.dtype),
        in_specs=[VMEM],
        out_specs=VMEM,
        scratch_shapes=[
            dma((dp - 1,)), dma((dp - 1,)), dma((mp - 1,)), dma((mp - 1,)), dma,
        ],
        compiler_params=pltpu.CompilerParams(collective_id=2, has_side_effects=True),
        name="stats",
    )(stats)


def local(
    embedded,
    targets,
    labels,
    counts,
    destinations,
    gain_in,
    w_query,
    w_key,
    w_value,
    w_out,
    gain_out,
    w_vocab,
    prev_probs,
    log_weights,
):
    dp = lax.axis_size("dp")
    mp = lax.axis_size("mp")
    data_index = lax.axis_index("dp")
    model_index = lax.axis_index("mp")
    chip = model_index // 2
    core = model_index % 2
    slots, seq_len, width = embedded.shape
    sequences = dp * slots // 2
    tokens = sequences * seq_len
    chips = mp // 2
    sibling = [(i, i ^ 1) for i in range(mp)]
    vocab_local = w_vocab.shape[1]
    columns = vocab_local // 2

    flat = embedded.reshape(slots * seq_len, width)
    given_columns = lax.dynamic_slice_in_dim(w_vocab, (1 - core) * columns, columns, 1)
    flat, given_columns = lax.optimization_barrier((flat, given_columns))
    taken_columns = lax.ppermute(given_columns, "mp", sibling)

    packed = jnp.concatenate([targets, labels[:, None], destinations[:, None]], axis=1)
    pad_rows, pad_columns = -slots % 8, -(seq_len + 2) % 128
    packed = jnp.pad(packed, ((0, pad_rows), (0, pad_columns)))
    full_rows, packed_all = gather_features(flat, packed, dp, mp)
    packed_all = packed_all[:, :slots].transpose(1, 0, 2).reshape(dp * slots, -1)
    is_live = (jnp.arange(slots)[:, None] < counts[None, :]).reshape(dp * slots)
    rank = jnp.cumsum(is_live.astype(jnp.int32)) - 1
    places = jnp.arange(sequences, dtype=jnp.int32)
    chosen = (rank[None, :] == places[:, None]) & is_live[None, :]
    entries = jnp.arange(dp * slots, dtype=jnp.int32)
    source = jnp.sum(jnp.where(chosen, entries[None, :], 0), axis=1).astype(jnp.int32)
    picked_ints = jnp.sum(jnp.where(chosen[:, :, None], packed_all[None], 0), axis=1)
    seq_targets = picked_ints[:, :seq_len]
    seq_labels = picked_ints[:, seq_len]
    seq_slots = picked_ints[:, seq_len + 1]

    mixed = attend(full_rows, gain_in, w_query, w_key, w_value, slots, seq_len)
    gain_part = lax.dynamic_slice_in_dim(gain_out, model_index * width, width, 0)
    final = project_output(mixed, w_out, flat, gain_part[None, :], mp)
    final = final.reshape(slots, seq_len, width)
    own_columns = lax.dynamic_slice_in_dim(w_vocab, core * columns, columns, 1)

    group = sequences // slots
    share = group // chips
    part = share * seq_len
    gathered = [
        lax.all_gather(final[j : j + 1], "dp", axis=0, tiled=True) for j in range(slots)
    ]

    def product(lhs, other):
        return jnp.dot(lhs, own_columns, preferred_element_type=jnp.float32) + jnp.dot(
            other, taken_columns, preferred_element_type=jnp.float32
        )

    ids = jnp.arange(columns, dtype=jnp.int32)
    tops, spreads, picks = [], [], []
    for j in range(slots):
        so_far = jnp.concatenate(gathered[: j + 1]) if j else gathered[0]
        order = jnp.roll(source[j * group : (j + 1) * group], -chip * share)
        rows = jnp.concatenate(
            [lax.dynamic_index_in_dim(so_far, order[i], 0, keepdims=True) for i in range(group)]
        ).reshape(group * seq_len, width)
        their_rows = lax.ppermute(rows, "mp", sibling)
        arrived = []
        for hop in range(1, chips):
            there = slice(hop * part, (hop + 1) * part)
            outgoing = product(rows[there], their_rows[there]).astype(jnp.bfloat16)
            across = [(i, (i + 2 * hop) % mp) for i in range(mp)]
            arrived.append(lax.ppermute(outgoing, "mp", across))
        logits = product(rows[:part], their_rows[:part])
        for piece in arrived:
            logits = logits + piece.astype(jnp.float32)
        goals = jnp.roll(seq_targets[j * group : (j + 1) * group], -chip * share, axis=0)
        goals = goals[:share].reshape(part) - (data_index * vocab_local + core * columns)
        top = jnp.max(logits, axis=1)
        tops.append(top)
        spreads.append(jnp.sum(jnp.exp(logits - top[:, None]), axis=1))
        picks.append(jnp.sum(jnp.where(ids[None, :] == goals[:, None], logits, 0.0), axis=1))
    stats = jnp.stack([jnp.concatenate(tops), jnp.concatenate(spreads), jnp.concatenate(picks)])
    stats = jnp.pad(stats, ((0, 5), (0, 0)))
    stats_all = gather_stats(stats, dp, mp).reshape(chips, 2 * dp, 8, slots * part)
    top_all = jnp.max(stats_all[:, :, 0], axis=1)
    scale = jnp.exp(stats_all[:, :, 0] - top_all[:, None])
    spread_all = jnp.sum(stats_all[:, :, 1] * scale, axis=1)
    picked_all = jnp.sum(stats_all[:, :, 2], axis=1)
    losses = top_all + jnp.log(spread_all) - picked_all
    losses = losses.reshape(chips, slots, part).transpose(1, 0, 2).reshape(sequences, seq_len)

    per_sequence = jnp.sum(losses, axis=1)
    domains = jnp.arange(DOMAINS, dtype=jnp.int32)
    member = (seq_labels[:, None] == domains[None, :]).astype(jnp.float32)
    loss_sums = jnp.sum(member * per_sequence[:, None], axis=0)
    token_tally = jnp.sum(member, axis=0) * seq_len
    placed = seq_slots[None, :] == places[:, None]
    losses = jnp.sum(jnp.where(placed[:, :, None], losses[None], 0.0), axis=1).reshape(tokens)
    block = tokens // (dp * mp)
    own_loss = lax.dynamic_slice_in_dim(
        losses, (data_index * mp + model_index) * block, block, 0
    )
    reward = loss_sums / jnp.maximum(token_tally, 1.0) / prev_probs
    new_weights = memory_rate * log_weights + (1.0 - memory_rate) * reward
    probs = (1.0 - DOMAINS * explore_mass) * jax.nn.softmax(step_rate * new_weights) + explore_mass
    return (own_loss, new_weights, probs)


def solution(mesh):
    placed = (
        P("dp", None, "mp"),
        P("dp", None),
        P("dp"),
        P(),
        P("dp"),
        P(),
        P(None, "mp"),
        P(None, "mp"),
        P(None, "mp"),
        P("mp", None),
        P(),
        P("mp", "dp"),
        P(),
        P(),
    )
    return jax.shard_map(
        local, mesh=mesh, in_specs=placed, out_specs=(P(("dp", "mp")), P(), P()), check_vma=False
    )
```

```python
import functools

import jax
import jax.numpy as jnp
from jax import lax
from jax.experimental import pallas as pl
from jax.experimental.pallas import tpu as pltpu
from jax.sharding import PartitionSpec as P

HEAD_DIM = 128
DOMAINS = 22
PIECES = 4
CHUNKS = 4
MESH = pl.DeviceIdType.MESH
VMEM = pl.BlockSpec(memory_space=pltpu.VMEM)

norm_eps = 1e-05
rope_base = 500000.0
memory_rate = 0.9
step_rate = 0.02
explore_mass = 0.005


def rotate_halves(tensor):
    full_width = tensor.shape[-1]
    half_width = full_width // 2
    frequency = jnp.power(
        jnp.float32(rope_base), -jnp.arange(half_width, dtype=jnp.float32) * 2.0 / full_width
    )
    angles = jnp.arange(tensor.shape[1], dtype=jnp.float32)[:, None] * frequency[None, :]
    cosine = jnp.cos(angles)[None, :, None, :]
    sine_part = jnp.sin(angles)[None, :, None, :]
    first_half = tensor[..., :half_width]
    second = tensor[..., half_width:]
    return jnp.concatenate(
        [first_half * cosine - second * sine_part, second * cosine + first_half * sine_part],
        axis=-1,
    )


def attend(full_rows, gain_in, w_query, w_key, w_value, seqs, seq_len):
    values = full_rows.astype(jnp.float32)
    inv_rms = lax.rsqrt(jnp.mean(values * values, axis=-1, keepdims=True) + norm_eps)
    normed = (values * inv_rms * gain_in).astype(jnp.bfloat16)
    local_heads = w_query.shape[1] // HEAD_DIM
    local_groups = w_key.shape[1] // HEAD_DIM
    group_size = local_heads // local_groups
    query = jnp.dot(normed, w_query, preferred_element_type=jnp.float32)
    key = jnp.dot(normed, w_key, preferred_element_type=jnp.float32)
    value = jnp.dot(normed, w_value, preferred_element_type=jnp.float32).astype(jnp.bfloat16)
    query = rotate_halves(query.reshape(seqs, seq_len, local_heads, HEAD_DIM))
    key = rotate_halves(key.reshape(seqs, seq_len, local_groups, HEAD_DIM))
    query = query.astype(jnp.bfloat16).reshape(seqs, seq_len, local_groups, group_size, HEAD_DIM)
    key = key.astype(jnp.bfloat16)
    value = value.reshape(seqs, seq_len, local_groups, HEAD_DIM)
    scores = jnp.einsum(
        "sqgre,skge->sgrqk", query, key, preferred_element_type=jnp.float32
    ) * HEAD_DIM ** (-0.5)
    causal = jnp.arange(seq_len)[:, None] >= jnp.arange(seq_len)[None, :]
    scores = jnp.where(causal, scores, -jnp.inf)
    weights = jax.nn.softmax(scores, axis=-1).astype(jnp.bfloat16)
    mixed = jnp.einsum("sgrqk,skge->sqgre", weights, value, preferred_element_type=jnp.float32)
    return mixed.astype(jnp.bfloat16).reshape(seqs * seq_len, local_heads * HEAD_DIM)


def remote(src, dst, send_sem, recv_sem, device):
    return pltpu.make_async_remote_copy(
        src_ref=src,
        dst_ref=dst,
        send_sem=send_sem,
        recv_sem=recv_sem,
        device_id=device,
        device_id_type=MESH,
    )


def greet(peers):
    barrier = pltpu.get_barrier_semaphore()
    for peer in peers:
        pl.semaphore_signal(barrier, inc=1, device_id=peer, device_id_type=MESH)
    pl.semaphore_wait(barrier, len(peers))


def features_kernel(
    dp, mp, x_ref, ints_ref, full_ref, all_ints_ref,
    across_send, across_recv, side_send, side_recv, int_send, int_recv, local_sem,
):
    d, m = lax.axis_index("dp"), lax.axis_index("mp")
    chips = mp // 2
    chip, core = m // 2, m % 2
    sibling = (d, chip * 2 + (1 - core))
    rows, width = x_ref.shape
    size = rows // PIECES
    far = [(d, lax.rem(chip + hop, chips) * 2 + core) for hop in range(1, chips)]
    around = [(lax.rem(d + k, dp), m) for k in range(1, dp)]
    greet([sibling] + far + around)

    def place(block, piece):
        start = pl.multiple_of(block * width, width)
        return full_ref.at[pl.ds(piece * size, size), pl.ds(start, width)]

    waits = []
    for piece in range(PIECES):
        for hop in range(1, chips):
            copy = remote(
                x_ref.at[pl.ds(piece * size, size)], place(m, piece),
                across_send.at[hop - 1, piece], across_recv.at[hop - 1, piece], far[hop - 1],
            )
            copy.start()
            waits.append(copy)
    sides = []
    for piece in range(PIECES):
        copy = remote(
            x_ref.at[pl.ds(piece * size, size)], place(m, piece),
            side_send.at[0, piece], side_recv.at[0, piece], sibling,
        )
        copy.start()
        sides.append(copy)
    ints = []
    for k in range(1, dp):
        copy = remote(
            ints_ref, all_ints_ref.at[d], int_send.at[k - 1], int_recv.at[k - 1], around[k - 1]
        )
        copy.start()
        ints.append(copy)
    locals_ = [
        pltpu.make_async_copy(ints_ref, all_ints_ref.at[d], local_sem.at[0]),
        pltpu.make_async_copy(
            x_ref, full_ref.at[:, pl.ds(pl.multiple_of(m * width, width), width)], local_sem.at[1]
        ),
    ]
    for copy in locals_:
        copy.start()
    at = 0
    for piece in range(PIECES):
        for hop in range(1, chips):
            waits[at].wait_recv()
            at += 1
            origin = lax.rem(chip + chips - hop, chips) * 2 + core
            copy = remote(
                place(origin, piece), place(origin, piece),
                side_send.at[hop, piece], side_recv.at[hop, piece], sibling,
            )
            copy.start()
            sides.append(copy)
    for copy in waits:
        copy.wait_send()
    for copy in sides + ints + locals_:
        copy.wait()


def gather_features(flat, ints, dp, mp):
    rows, width = flat.shape
    chips = mp // 2
    dma = pltpu.SemaphoreType.DMA
    return pl.pallas_call(
        functools.partial(features_kernel, dp, mp),
        out_shape=(
            jax.ShapeDtypeStruct((rows, width * mp), flat.dtype),
            jax.ShapeDtypeStruct((dp,) + ints.shape, ints.dtype),
        ),
        in_specs=[VMEM] * 2,
        out_specs=(VMEM, VMEM),
        scratch_shapes=[
            dma((chips - 1, PIECES)), dma((chips - 1, PIECES)),
            dma((chips, PIECES)), dma((chips, PIECES)),
            dma((dp - 1,)), dma((dp - 1,)), dma((2,)),
        ],
        compiler_params=pltpu.CompilerParams(collective_id=0, has_side_effects=True),
        name="features",
    )(flat, ints)


def output_kernel(
    mp, mixed_ref, w_ref, own_ref, gain_ref, final_ref,
    side_out, side_in, far_out, far_in, kept, total, square_out, square_in,
    side_send, side_recv, far_send, far_recv, square_send, square_recv,
):
    d, m = lax.axis_index("dp"), lax.axis_index("mp")
    chips = mp // 2
    chip, core = m // 2, m % 2
    sibling = (d, chip * 2 + (1 - core))
    rows, width = own_ref.shape
    size = rows // PIECES
    peers = [(d, lax.rem(m + k, mp)) for k in range(1, mp)]
    greet(peers)
    hops = list(range(1, chips)) + [0]
    target = [lax.rem(chip + hop, chips) for hop in range(chips)]

    def product(block):
        start = pl.multiple_of(block * width, width)
        return jnp.dot(
            mixed_ref[...], w_ref[:, pl.ds(start, width)], preferred_element_type=jnp.float32
        )

    def cut(piece):
        return pl.ds(piece * size, size)

    sides = {}
    for hop in hops:
        side_out[hop] = product(target[hop] * 2 + (1 - core)).astype(jnp.bfloat16)
        for piece in range(PIECES):
            sides[hop, piece] = remote(
                side_out.at[hop, cut(piece)], side_in.at[hop, cut(piece)],
                side_send.at[hop, piece], side_recv.at[hop, piece], sibling,
            )
            sides[hop, piece].start()
    for hop in hops:
        kept[hop] = product(target[hop] * 2 + core)
    fars = {}
    for piece in range(PIECES):
        for hop in range(1, chips):
            sides[hop, piece].wait_recv()
            far_out[hop - 1, cut(piece)] = (
                kept[hop, cut(piece)] + side_in[hop, cut(piece)].astype(jnp.float32)
            ).astype(jnp.bfloat16)
            fars[hop, piece] = remote(
                far_out.at[hop - 1, cut(piece)], far_in.at[hop - 1, cut(piece)],
                far_send.at[hop - 1, piece], far_recv.at[hop - 1, piece],
                (d, target[hop] * 2 + core),
            )
            fars[hop, piece].start()
    for piece in range(PIECES):
        sides[0, piece].wait_recv()
        value = kept[0, cut(piece)] + side_in[0, cut(piece)].astype(jnp.float32)
        for hop in range(1, chips):
            fars[hop, piece].wait_recv()
            value = value + far_in[hop - 1, cut(piece)].astype(jnp.float32)
        total[cut(piece)] = value + own_ref[cut(piece)].astype(jnp.float32)
    hidden = total[...]
    squares = jnp.sum(hidden * hidden, axis=1, keepdims=True)
    square_out[...] = jnp.transpose(jnp.broadcast_to(squares, (rows, 128)))[:8]
    swaps = []
    for k in range(1, mp):
        copy = remote(
            square_out, square_in.at[k - 1],
            square_send.at[k - 1], square_recv.at[k - 1], peers[k - 1],
        )
        copy.start()
        swaps.append(copy)
    for copy in swaps:
        copy.wait()
    summed = square_out[...]
    for k in range(mp - 1):
        summed = summed + square_in[k]
    inverse = lax.rsqrt(summed / (width * mp) + norm_eps)
    inverse = jnp.transpose(jnp.concatenate([inverse] * 16, axis=0))[:, :1]
    final_ref[...] = (total[...] * inverse * gain_ref[...]).astype(final_ref.dtype)
    for copy in list(sides.values()) + list(fars.values()):
        copy.wait_send()


def project_output(mixed, w_out, own, gain_part, mp):
    rows, width = own.shape
    chips = mp // 2
    dma = pltpu.SemaphoreType.DMA
    half = jnp.bfloat16
    return pl.pallas_call(
        functools.partial(output_kernel, mp),
        out_shape=jax.ShapeDtypeStruct(own.shape, half),
        in_specs=[VMEM] * 4,
        out_specs=VMEM,
        scratch_shapes=[
            pltpu.VMEM((chips, rows, width), half),
            pltpu.VMEM((chips, rows, width), half),
            pltpu.VMEM((chips - 1, rows, width), half),
            pltpu.VMEM((chips - 1, rows, width), half),
            pltpu.VMEM((chips, rows, width), jnp.float32),
            pltpu.VMEM((rows, width), jnp.float32),
            pltpu.VMEM((8, rows), jnp.float32),
            pltpu.VMEM((mp - 1, 8, rows), jnp.float32),
            dma((chips, PIECES)), dma((chips, PIECES)),
            dma((chips - 1, PIECES)), dma((chips - 1, PIECES)),
            dma((mp - 1,)), dma((mp - 1,)),
        ],
        compiler_params=pltpu.CompilerParams(collective_id=1, has_side_effects=True),
        name="output",
    )(mixed, w_out, own, gain_part)


def stats_kernel(dp, mp, x_ref, all_ref, dp_send, dp_recv, mp_send, mp_recv, local_sem):
    d, m = lax.axis_index("dp"), lax.axis_index("mp")
    around = [(lax.rem(d + k, dp), m) for k in range(1, dp)]
    beside = [(d, lax.rem(m + k, mp)) for k in range(1, mp)]
    greet(around + beside)
    first = []
    for k in range(1, dp):
        copy = remote(
            x_ref, all_ref.at[m, d], dp_send.at[k - 1], dp_recv.at[k - 1], around[k - 1]
        )
        copy.start()
        first.append(copy)
    here = pltpu.make_async_copy(x_ref, all_ref.at[m, d], local_sem)
    here.start()
    here.wait()
    for copy in first:
        copy.wait()
    second = []
    for k in range(1, mp):
        copy = remote(
            all_ref.at[m], all_ref.at[m], mp_send.at[k - 1], mp_recv.at[k - 1], beside[k - 1]
        )
        copy.start()
        second.append(copy)
    for copy in second:
        copy.wait()


def gather_stats(stats, dp, mp):
    dma = pltpu.SemaphoreType.DMA
    return pl.pallas_call(
        functools.partial(stats_kernel, dp, mp),
        out_shape=jax.ShapeDtypeStruct((mp, dp) + stats.shape, stats.dtype),
        in_specs=[VMEM],
        out_specs=VMEM,
        scratch_shapes=[
            dma((dp - 1,)), dma((dp - 1,)), dma((mp - 1,)), dma((mp - 1,)), dma,
        ],
        compiler_params=pltpu.CompilerParams(collective_id=2, has_side_effects=True),
        name="stats",
    )(stats)


def rows_kernel(
    dp, order_ref, x_ref, rows_ref, all_ref, mate_send, mate_recv, line_send, line_recv, local_sem
):
    d, m = lax.axis_index("dp"), lax.axis_index("mp")
    slots = x_ref.shape[0]
    length = dp // 2
    where, side = d // 2, d % 2
    mate = where * 2 + (1 - side)
    after = [lax.rem(where + k, length) for k in range(length)]
    before = [lax.rem(where + length - k, length) for k in range(length)]
    line = [(after[k] * 2 + side, m) for k in range(1, length)]
    greet([(mate, m)] + line)

    def place(block, slot):
        return all_ref.at[block * slots + slot]

    def to_mate(src, block, k, slot):
        copy = remote(
            src, place(block, slot), mate_send.at[k, slot], mate_recv.at[k, slot], (mate, m)
        )
        copy.start()
        return copy

    def to_line(src, block, k, turn, slot):
        copy = remote(
            src, place(block, slot), line_send.at[turn, k - 1, slot],
            line_recv.at[turn, k - 1, slot], line[k - 1],
        )
        copy.start()
        return copy

    mates, lines = {}, {}
    here = pltpu.make_async_copy(x_ref, all_ref.at[pl.ds(d * slots, slots)], local_sem)
    here.start()
    for slot in range(slots):
        mates[0, slot] = to_mate(x_ref.at[slot], d, 0, slot)
        for k in range(1, length):
            lines[0, k, slot] = to_line(x_ref.at[slot], d, k, 0, slot)
    for slot in range(slots):
        if slot % 2:
            mates[0, slot].wait_recv()
            for k in range(1, length):
                lines[1, k, slot] = to_line(place(mate, slot), mate, k, 1, slot)
        else:
            for k in range(1, length):
                lines[0, k, slot].wait_recv()
                block = before[k] * 2 + side
                mates[k, slot] = to_mate(place(block, slot), block, k, slot)
    here.wait()
    for (k, slot), copy in mates.items():
        if slot % 2 and k == 0:
            copy.wait_send()
        else:
            copy.wait()
    for (turn, k, slot), copy in lines.items():
        if slot % 2 == 0 and turn == 0:
            copy.wait_send()
        else:
            copy.wait()
    for i in range(rows_ref.shape[0]):
        rows_ref[i] = all_ref[order_ref[i]]


def gather_rows(order, final, dp):
    slots, seq_len, width = final.shape
    dma = pltpu.SemaphoreType.DMA
    length = dp // 2
    return pl.pallas_call(
        functools.partial(rows_kernel, dp),
        out_shape=jax.ShapeDtypeStruct((order.shape[0], seq_len, width), final.dtype),
        in_specs=[pl.BlockSpec(memory_space=pltpu.SMEM), VMEM],
        out_specs=VMEM,
        scratch_shapes=[
            pltpu.VMEM((dp * slots, seq_len, width), final.dtype),
            dma((length, slots)), dma((length, slots)),
            dma((2, length - 1, slots)), dma((2, length - 1, slots)), dma,
        ],
        compiler_params=pltpu.CompilerParams(collective_id=3, has_side_effects=True),
        name="rows",
    )(order, final)


def local(
    embedded,
    targets,
    labels,
    counts,
    destinations,
    gain_in,
    w_query,
    w_key,
    w_value,
    w_out,
    gain_out,
    w_vocab,
    prev_probs,
    log_weights,
):
    dp = lax.axis_size("dp")
    mp = lax.axis_size("mp")
    data_index = lax.axis_index("dp")
    model_index = lax.axis_index("mp")
    chip = model_index // 2
    core = model_index % 2
    slots, seq_len, width = embedded.shape
    sequences = dp * slots // 2
    tokens = sequences * seq_len
    chips = mp // 2
    sibling = [(i, i ^ 1) for i in range(mp)]
    vocab_local = w_vocab.shape[1]
    columns = vocab_local // 2

    flat = embedded.reshape(slots * seq_len, width)
    given_columns = lax.dynamic_slice_in_dim(w_vocab, (1 - core) * columns, columns, 1)
    taken_columns = lax.ppermute(given_columns, "mp", sibling)
    own_columns = lax.dynamic_slice_in_dim(w_vocab, core * columns, columns, 1)

    packed = jnp.concatenate([targets, labels[:, None], destinations[:, None]], axis=1)
    pad_rows, pad_columns = -slots % 8, -(seq_len + 2) % 128
    packed = jnp.pad(packed, ((0, pad_rows), (0, pad_columns)))
    full_rows, packed_all = gather_features(flat, packed, dp, mp)
    packed_all = packed_all[:, :slots].reshape(dp * slots, -1)
    entries = jnp.arange(dp * slots, dtype=jnp.int32)
    is_live = entries % slots < counts[entries // slots]
    places = jnp.arange(sequences, dtype=jnp.int32)
    chosen = (packed_all[:, seq_len + 1][None, :] == places[:, None]) & is_live[None, :]
    source = jnp.sum(jnp.where(chosen, entries[None, :], 0), axis=1).astype(jnp.int32)
    picked_ints = jnp.sum(jnp.where(chosen[:, :, None], packed_all[None], 0), axis=1)
    seq_targets = picked_ints[:, :seq_len]
    seq_labels = picked_ints[:, seq_len]
    seq_part = sequences // chips
    order = jnp.roll(source, -chip * seq_part)

    mixed = attend(full_rows, gain_in, w_query, w_key, w_value, slots, seq_len)
    gain_part = lax.dynamic_slice_in_dim(gain_out, model_index * width, width, 0)
    final = project_output(mixed, w_out, flat, gain_part[None, :], mp)
    final = final.reshape(slots, seq_len, width)
    rows = gather_rows(order, final, dp).reshape(tokens, width)
    their_rows = lax.ppermute(rows, "mp", sibling)
    part = tokens // chips
    goals = jnp.roll(seq_targets, -chip * seq_part, axis=0)[:seq_part].reshape(part)
    goals = goals - (data_index * vocab_local + core * columns)

    def product(lhs, other, start, size):
        return jnp.dot(
            lhs, own_columns[:, start : start + size], preferred_element_type=jnp.float32
        ) + jnp.dot(
            other, taken_columns[:, start : start + size], preferred_element_type=jnp.float32
        )

    size = columns // CHUNKS
    arrived = []
    for i in range(CHUNKS):
        hops = []
        for hop in range(1, chips):
            there = slice(hop * part, (hop + 1) * part)
            outgoing = product(rows[there], their_rows[there], i * size, size)
            across = [(j, (j + 2 * hop) % mp) for j in range(mp)]
            hops.append(lax.ppermute(outgoing.astype(jnp.bfloat16), "mp", across))
        arrived.append(hops)
    tops, spreads, picks = [], [], []
    for i in range(CHUNKS):
        logits = product(rows[:part], their_rows[:part], i * size, size)
        for piece in arrived[i]:
            logits = logits + piece.astype(jnp.float32)
        top = jnp.max(logits, axis=1)
        tops.append(top)
        spreads.append(jnp.sum(jnp.exp(logits - top[:, None]), axis=1))
        ids = i * size + jnp.arange(size, dtype=jnp.int32)
        picks.append(jnp.sum(jnp.where(ids[None, :] == goals[:, None], logits, 0.0), axis=1))
    top = functools.reduce(jnp.maximum, tops)
    spread = sum(own * jnp.exp(high - top) for own, high in zip(spreads, tops))
    stats = jnp.pad(jnp.stack([top, spread, sum(picks)]), ((0, 5), (0, 0)))
    stats_all = gather_stats(stats, dp, mp).reshape(chips, 2 * dp, 8, part)
    top_all = jnp.max(stats_all[:, :, 0], axis=1)
    scale = jnp.exp(stats_all[:, :, 0] - top_all[:, None])
    spread_all = jnp.sum(stats_all[:, :, 1] * scale, axis=1)
    picked_all = jnp.sum(stats_all[:, :, 2], axis=1)
    losses = (top_all + jnp.log(spread_all) - picked_all).reshape(sequences, seq_len)

    per_sequence = jnp.sum(losses, axis=1)
    domains = jnp.arange(DOMAINS, dtype=jnp.int32)
    member = (seq_labels[:, None] == domains[None, :]).astype(jnp.float32)
    loss_sums = jnp.sum(member * per_sequence[:, None], axis=0)
    token_tally = jnp.sum(member, axis=0) * seq_len
    losses = losses.reshape(tokens)

    block = tokens // (dp * mp)
    own_loss = lax.dynamic_slice_in_dim(
        losses, (data_index * mp + model_index) * block, block, 0
    )
    reward = loss_sums / jnp.maximum(token_tally, 1.0) / prev_probs
    new_weights = memory_rate * log_weights + (1.0 - memory_rate) * reward
    probs = (1.0 - DOMAINS * explore_mass) * jax.nn.softmax(step_rate * new_weights) + explore_mass
    return (own_loss, new_weights, probs)


def solution(mesh):
    placed = (
        P("dp", None, "mp"),
        P("dp", None),
        P("dp"),
        P(),
        P("dp"),
        P(),
        P(None, "mp"),
        P(None, "mp"),
        P(None, "mp"),
        P("mp", None),
        P(),
        P("mp", "dp"),
        P(),
        P(),
    )
    return jax.shard_map(
        local, mesh=mesh, in_specs=placed, out_specs=(P(("dp", "mp")), P(), P()), check_vma=False
    )
```
